32 devices in a mesh: band: 16 (over z, y, x), lev: 2 (over core).
Axes of the slice: x: 2, y: 2, z: 4, core: 2. Of those that a mesh axis runs over, the one named last changes fastest.
Arguments:
- arrival_adjoint: bfloat16 [160, 64, 1536], P('band', 'lev'), may hold values from -6 to 6
- interp_tiles: bfloat16 [160, 12, 128, 128], P('band'), may hold values from -0.5 to 0.5
- departure_block: int32 [160, 12], P('band'), may hold values from 0 to 239
- slot_wavenumber: int32 [768], replicated, may hold values from 0 to 767, each once
- legendre: bfloat16 [768, 160, 768], P('band', None, 'lev'), may hold values from -0.5 to 0.5
Outputs:
- spectral: bfloat16 [768, 64, 2, 768], P('band', None, None, 'lev')
The draws below stay inside these ranges and needn't reach their ends.
Inputs may be any that keep to these rules, and one draw needn't show every extreme that they name: `departure_block`: an entry d of the tile at latitude l names latitude L + d // 12 - 5 and longitude block d % 12, where L is the first latitude of l's band of 10. `slot_wavenumber`: each wavenumber below 768 stands in exactly one slot.
All inputs are finite; a program needn't handle non-finite values.
Results may differ from the reference program's by a relative error of at most 0.015.
Values may be sent and summed in bfloat16 or wider, within the bound.
No kernel may reach another device: no remote copies, remote signals or barrier semaphores. Data moves between devices by JAX's collectives and lax.ppermute only.
A program may use at most 128 MiB of HBM per device.

```python
import math
import jax
import jax.numpy as jnp
from jax import lax

LAT_DEV = 10
HALO = 5
TILE = 128
LON = 1536
M = 768
LEVELS = 64
NBLK = 12
NLAT = 160


def with_ends(values, stream_key, least, top_value):
    longest = values.shape.index(max(values.shape))
    spots = []
    for shift in (0, 1):
        where = [jax.random.randint(jax.random.fold_in(stream_key, axis), (), 0, length) for axis, length in enumerate(values.shape)]
        where[longest] = (where[longest] + shift) % values.shape[longest]
        spots.append(tuple(where))
    return values.at[spots[0]].set(least).at[spots[1]].set(top_value)


def block_scale(own_key, dims, cuts, low, largest):
    gain, own = 1.0, jax.random.fold_in(own_key, 6)
    for axis_at, blocks in cuts:
        heights = jnp.exp(jax.random.uniform(jax.random.fold_in(own, axis_at), (blocks,), jnp.float32, low / len(cuts), largest / len(cuts)))
        gain = gain * jnp.repeat(heights, dims[axis_at] // blocks).reshape([-1 if axis == axis_at else 1 for axis in range(len(dims))])
    return gain


def normal_values(key, shape, spread, most, shards=(), kind=jnp.bfloat16):
    drawn = spread * jax.random.normal(key, shape, jnp.float32)
    if shards:
        drawn = drawn * block_scale(key, shape, shards, -0.22, 0.18)
    return jnp.clip(drawn, -most, most).astype(kind)


def setup_inputs(seed: int = 0) -> dict:
    keys = jax.random.split(jax.random.key(seed), 6)
    return {
        "arrival_adjoint": normal_values(keys[0], (NLAT, LEVELS, LON), 1.0, 6.0, ((0, 16), (1, 2))),
        "interp_tiles": normal_values(keys[1], (NLAT, NBLK, TILE, TILE), TILE ** -0.5, 0.5, ((0, 16),)),
        "departure_block": with_ends(jax.random.randint(keys[2], (NLAT, NBLK), 0, (LAT_DEV + 2 * HALO) * NBLK), jax.random.fold_in(keys[2], 1), 0, ((LAT_DEV + 2 * HALO) * NBLK) - 1).astype(jnp.int32),
        "slot_wavenumber": jax.random.permutation(keys[3], M).astype(jnp.int32),
        "legendre": normal_values(keys[4], (M, NLAT, M), NLAT ** -0.5, 0.5, ((0, 16), (2, 2))),
    }


def wave_table(slot_wavenumber, lon_count):
    column = jnp.arange(lon_count, dtype=jnp.int32)[:, None]
    product = column * slot_wavenumber[None, :] % lon_count
    angle = product.astype(jnp.float32) * (2.0 * math.pi / lon_count)
    factor = math.sqrt(2.0 / lon_count)
    return jnp.stack([jnp.cos(angle) * factor, jnp.sin(angle) * factor]).astype(jnp.bfloat16)

def reference(arrival_adjoint, interp_tiles, departure_block, slot_wavenumber, legendre):
    tiles = arrival_adjoint.reshape(NLAT, LEVELS, NBLK, TILE).astype(jnp.float32)
    contrib = jnp.einsum('lvbi,lbik->lbvk', tiles, interp_tiles.astype(jnp.float32), precision=lax.Precision.HIGHEST)
    latitude = jnp.arange(NLAT, dtype=jnp.int32)[:, None]
    row = latitude // LAT_DEV * LAT_DEV + departure_block // NBLK
    segment = (row * NBLK + departure_block % NBLK).astype(jnp.int32)
    padded = jax.ops.segment_sum(contrib.reshape(NLAT * NBLK, LEVELS * TILE), segment.reshape(-1), num_segments=(NLAT + 2 * HALO) * NBLK)
    grid = padded.reshape(NLAT + 2 * HALO, NBLK, LEVELS, TILE)[HALO:HALO + NLAT].astype(jnp.bfloat16)
    table = wave_table(slot_wavenumber, LON).reshape(2, NBLK, TILE, M)
    fourier = jnp.einsum('lbvt,cbts->scvl', grid.astype(jnp.float32), table.astype(jnp.float32), precision=lax.Precision.HIGHEST).astype(jnp.bfloat16)
    degree = jnp.arange(M, dtype=jnp.int32)

    def one_slot(inputs):
        block, tables, wave = inputs
        result = jnp.einsum('cvl,ln->vcn', block.astype(jnp.float32), tables.astype(jnp.float32), precision=lax.Precision.HIGHEST)
        return jnp.where(degree[None, None, :] >= wave, result, 0.0).astype(jnp.bfloat16)
    return lax.map(one_slot, (fourier, legendre, slot_wavenumber))
```

```python
import functools
import math

import jax
import jax.numpy as jnp
from jax import lax
from jax.experimental import pallas as pl
from jax.experimental.pallas import tpu as pltpu
from jax.sharding import PartitionSpec as P

BF = jnp.bfloat16
F32 = jnp.float32
LANES = 128
VMEM_LIMIT = 48 * 2**20


def passed_along(block, axis, distance):
    devices = range(lax.axis_size(axis))
    route = [(i - distance, i) for i in devices if i - distance in devices]
    return lax.ppermute(block, axis, route)


def whole(shape):
    return pl.BlockSpec(shape, lambda *_: (0,) * len(shape))


def interpolate_kernel(rim, depart, arrival, tiles, below, mid, above, sums):
    lat = pl.program_id(0)
    blocks, width = tiles.shape[1], tiles.shape[2]

    @pl.when(lat == 0)
    def _():
        sums[...] = jnp.zeros_like(sums)

    contrib = [
        jnp.dot(
            arrival[0, :, b * width : (b + 1) * width], tiles[0, b], preferred_element_type=F32
        )
        for b in range(blocks)
    ]
    for b in range(blocks):
        target = depart[lat * blocks + b]
        sums[target] += contrib[b]

    @pl.when(lat == pl.num_programs(0) - 1)
    def _():
        below[...] = sums[:rim].astype(BF)
        above[...] = sums[sums.shape[0] - rim :].astype(BF)
        mid[...] = sums[rim : sums.shape[0] - rim]


def interpolate(arrival, tiles, depart):
    lats, levels, lons = arrival.shape
    blocks, width = tiles.shape[1], tiles.shape[2]
    rim = lats // 2 * blocks
    segments = lats * blocks + 2 * rim
    grid_spec = pltpu.PrefetchScalarGridSpec(
        num_scalar_prefetch=1,
        grid=(lats,),
        in_specs=[
            pl.BlockSpec((1, levels, lons), lambda i, d: (i, 0, 0)),
            pl.BlockSpec((1, blocks, width, width), lambda i, d: (i, 0, 0, 0)),
        ],
        out_specs=[
            whole((rim, levels, width)),
            whole((segments - 2 * rim, levels, width)),
            whole((rim, levels, width)),
        ],
        scratch_shapes=[pltpu.VMEM((segments, levels, width), F32)],
    )
    return pl.pallas_call(
        functools.partial(interpolate_kernel, rim),
        grid_spec=grid_spec,
        out_shape=[
            jax.ShapeDtypeStruct((rim, levels, width), BF),
            jax.ShapeDtypeStruct((segments - 2 * rim, levels, width), F32),
            jax.ShapeDtypeStruct((rim, levels, width), BF),
        ],
        compiler_params=pltpu.CompilerParams(vmem_limit_bytes=VMEM_LIMIT),
        cost_estimate=pl.CostEstimate(
            flops=2 * lats * levels * lons * width,
            bytes_accessed=2 * (arrival.size + tiles.size),
            transcendentals=0,
        ),
        name="interpolate",
    )(depart.reshape(-1), arrival, tiles)


def table_kernel(lons, waves, table):
    blocks = lons // LANES
    rows = waves.shape[1]
    wave = waves[0].astype(F32)
    lane = lax.broadcasted_iota(jnp.int32, (rows, LANES), 1).astype(F32)
    product = lane * wave

    def turn(steps, period):
        left = steps - period * jnp.floor((steps + 0.5) * (1.0 / period))
        angle = left * (2.0 * math.pi / period)
        return jnp.cos(angle), jnp.sin(angle)

    fine_cos, fine_sin = turn(product, float(lons))
    coarse_cos, coarse_sin = turn(product, float(blocks))
    factor = math.sqrt(2.0 / lons)
    coarse_cos = coarse_cos * factor
    coarse_sin = coarse_sin * factor
    for b in range(blocks):
        cos_b, sin_b = coarse_cos[:, b : b + 1], coarse_sin[:, b : b + 1]
        at = slice(b * LANES, (b + 1) * LANES)
        table[0, 0, :, at] = (cos_b * fine_cos - sin_b * fine_sin).astype(BF)
        table[0, 1, :, at] = (sin_b * fine_cos + cos_b * fine_sin).astype(BF)


def wave_table(waves, lons):
    halves, count, _ = waves.shape
    rows = 128
    return pl.pallas_call(
        functools.partial(table_kernel, lons),
        grid=(halves, count // rows),
        in_specs=[pl.BlockSpec((1, rows, 1), lambda h, i: (h, i, 0))],
        out_specs=pl.BlockSpec((1, 2, rows, lons), lambda h, i: (h, 0, i, 0)),
        out_shape=jax.ShapeDtypeStruct((halves, 2, count, lons), BF),
        compiler_params=pltpu.CompilerParams(vmem_limit_bytes=VMEM_LIMIT),
        cost_estimate=pl.CostEstimate(
            flops=40 * halves * count * lons, bytes_accessed=4 * halves * count * lons, transcendentals=0
        ),
        name="table",
    )(waves)


def fourier_kernel(mid, from_below, from_above, table, sent, grid, sums):
    segments, levels, width = mid.shape
    rim = from_below.shape[0]
    lats, _ = sent.shape[1], sent.shape[3]
    blocks = segments // lats
    per_row = LANES // levels
    parts = table.shape[0]
    groups = pl.cdiv(lats, per_row)
    half = sent.shape[2]

    @pl.when(pl.program_id(0) == 0)
    def _():
        for lat in range(groups * per_row):
            group, place = lat // per_row, lat % per_row
            for b in range(blocks):
                seg = lat * blocks + b
                if lat >= lats:
                    row = jnp.zeros((levels, width), BF)
                else:
                    add = from_below[seg] if seg < rim else from_above[seg - rim]
                    row = (mid[seg] + add.astype(F32)).astype(BF)
                for k in range(parts):
                    start = group * LANES + (place + k) % per_row * levels
                    grid[k, start : start + levels, b * width : (b + 1) * width] = row

    for k in range(parts):
        sums[k] = lax.dot_general(
            table[k], grid[k], (((1,), (1,)), ((), ())), preferred_element_type=F32
        )
    lane = lax.broadcasted_iota(jnp.int32, (half, LANES), 1) // levels
    for d in range(sent.shape[0]):
        for group in range(groups):
            held = [
                sums[k, d * half : (d + 1) * half, group * LANES : (group + 1) * LANES]
                for k in range(parts)
            ]
            for place in range(per_row):
                lat = group * per_row + place
                if lat >= lats:
                    continue
                row = held[(0 - place) % per_row]
                for p in range(1, per_row):
                    row = jnp.where(lane == p, held[(p - place) % per_row], row)
                if place:
                    row = pltpu.roll(row, LANES - place * levels, 1)
                sent[d, lat] = row.astype(BF)


def fourier(mid, from_below, from_above, table, bands):
    segments, levels, width = mid.shape
    halves, _, count, lons = table.shape
    lats = segments * width // lons
    half = count // bands
    parts = 2 * halves
    steps = 2
    rows = count // steps
    groups = pl.cdiv(lats * levels, LANES)
    return pl.pallas_call(
        fourier_kernel,
        grid=(steps,),
        in_specs=[
            whole(mid.shape),
            whole(from_below.shape),
            whole(from_above.shape),
            pl.BlockSpec((parts, rows, lons), lambda i: (0, i, 0)),
        ],
        out_specs=pl.BlockSpec((bands // steps, lats, half, LANES), lambda i: (i, 0, 0, 0)),
        out_shape=jax.ShapeDtypeStruct((bands, lats, half, LANES), BF),
        scratch_shapes=[
            pltpu.VMEM((parts, groups * LANES, lons), BF),
            pltpu.VMEM((parts, rows, groups * LANES), F32),
        ],
        compiler_params=pltpu.CompilerParams(vmem_limit_bytes=VMEM_LIMIT),
        cost_estimate=pl.CostEstimate(
            flops=4 * halves * count * lons * lats * levels,
            bytes_accessed=4 * halves * count * lons,
            transcendentals=0,
        ),
        name="fourier",
    )(mid, from_below, from_above, table.reshape(parts, count, lons))


def legendre_kernel(per_step, waves, place, own, other, leg_a, leg_b, out, first, second):
    step = pl.program_id(0)
    lats, half, lanes = own.shape
    levels = lanes // 4
    degrees = leg_a.shape[2]
    lev = place[0]

    @pl.when(step == 0)
    def _():
        @pl.when(lev == 0)
        def _():
            first[...] = own[...].astype(F32).reshape(first.shape)
            second[...] = other[...].astype(F32).reshape(first.shape)

        @pl.when(lev != 0)
        def _():
            first[...] = other[...].astype(F32).reshape(first.shape)
            second[...] = own[...].astype(F32).reshape(first.shape)

    lane = lax.broadcasted_iota(jnp.int32, (lats, lanes), 1)
    column = lax.broadcasted_iota(jnp.int32, (levels, degrees), 1) + lev * degrees
    for i in range(per_step):
        r = step * per_step + i
        x0 = first[pl.ds(r, lats, stride=half), :]
        x1 = second[pl.ds(r, lats, stride=half), :]
        for slot in range(2):
            low, high = (x0, x1) if slot == 0 else (x1, x0)
            joined = jnp.where(lane < lanes // 2, low, high).astype(BF)
            leg = (leg_a, leg_b)[slot][i]
            sums = lax.dot_general(
                joined, leg, (((0,), (0,)), ((), ())), preferred_element_type=F32
            )
            keep = column >= waves[slot * half + r]
            for side in range(2):
                for part in range(2):
                    at = (side * 2 + part) * levels
                    level = (side ^ slot) * levels
                    out[slot, i, level : level + levels, part, :] = jnp.where(
                        keep, sums[at : at + levels], 0.0
                    ).astype(BF)


def legendre_sums(own, other, legendre, waves, lev):
    slots, lats, degrees = legendre.shape
    half, lanes = slots // 2, own.shape[3]
    per_step = math.gcd(half, 4)
    shape = (lats, half, lanes)
    grid_spec = pltpu.PrefetchScalarGridSpec(
        num_scalar_prefetch=2,
        grid=(half // per_step,),
        in_specs=[
            whole(shape),
            whole(shape),
            pl.BlockSpec((per_step, lats, degrees), lambda i, *_: (i, 0, 0)),
            pl.BlockSpec((per_step, lats, degrees), lambda i, *_: (i + half // per_step, 0, 0)),
        ],
        out_specs=pl.BlockSpec(
            (2, per_step, lanes // 2, 2, degrees), lambda i, *_: (0, i, 0, 0, 0)
        ),
        scratch_shapes=[
            pltpu.VMEM((lats * half, lanes), F32),
            pltpu.VMEM((lats * half, lanes), F32),
        ],
    )
    out = pl.pallas_call(
        functools.partial(legendre_kernel, per_step),
        grid_spec=grid_spec,
        out_shape=jax.ShapeDtypeStruct((2, half, lanes // 2, 2, degrees), BF),
        compiler_params=pltpu.CompilerParams(vmem_limit_bytes=VMEM_LIMIT),
        cost_estimate=pl.CostEstimate(
            flops=2 * slots * lats * lanes * degrees,
            bytes_accessed=2 * legendre.size + 2 * slots * lanes * degrees,
            transcendentals=0,
        ),
        name="legendre_sums",
    )(waves, lev, own.reshape(shape), other.reshape(shape), legendre, legendre)
    return out.reshape(slots, lanes // 2, 2, degrees)


def local(arrival_adjoint, interp_tiles, departure_block, slot_wavenumber, legendre):
    lons = arrival_adjoint.shape[2]
    slots = legendre.shape[0]
    bands = lax.axis_size("band")
    lev = lax.axis_index("lev")
    to_below, mid, to_above = interpolate(arrival_adjoint, interp_tiles, departure_block)
    from_below = passed_along(to_above, "band", 1)
    from_above = passed_along(to_below, "band", -1)
    pairs = slot_wavenumber.reshape(bands, 2, slots // 2).transpose(1, 0, 2)
    pairs = jnp.where(lev == 0, pairs, pairs[::-1])
    table = wave_table(pairs.reshape(2, -1, 1), lons)
    sent = fourier(mid, from_below, from_above, table, bands)
    own = lax.all_to_all(sent, "band", split_axis=0, concat_axis=0)
    other = lax.ppermute(own, "lev", [(0, 1), (1, 0)])
    waves = lax.dynamic_slice_in_dim(slot_wavenumber, lax.axis_index("band") * slots, slots)
    return legendre_sums(own, other, legendre, waves, lev.reshape(1))


def solution(mesh):
    placed = (
        P("band", "lev", None),
        P("band", None, None, None),
        P("band", None),
        P(),
        P("band", None, "lev"),
    )
    return jax.shard_map(
        local, mesh=mesh, in_specs=placed, out_specs=P("band", None, None, "lev"), check_vma=False
    )
```

```python
import functools
import math

import jax
import jax.numpy as jnp
from jax import lax
from jax.experimental import pallas as pl
from jax.experimental.pallas import tpu as pltpu
from jax.sharding import PartitionSpec as P

BF = jnp.bfloat16
F32 = jnp.float32
LANES = 128
MIB = 2**20
A_LIMIT = 56 * MIB
T_LIMIT = 44 * MIB
VMEM = pl.BlockSpec(memory_space=pltpu.VMEM)
ANY = pl.BlockSpec(memory_space=pl.ANY)


def exchanged(block, pairs):
    return lax.ppermute(block, "band", pairs + [(j, i) for i, j in pairs])


def interpolate_kernel(
    rim, odd, depart, arrival, tiles, first, second, mid, rows, weights, sums, landed
):
    lats, blocks, width = tiles.shape[0], tiles.shape[1], tiles.shape[2]
    whole_rows = pltpu.make_async_copy(arrival, rows, landed.at[0])
    whole_rows.start()
    split = lats // 2
    halves = []
    for i, some in enumerate((slice(0, split), slice(split, lats))):
        halves.append(pltpu.make_async_copy(tiles.at[some], weights.at[some], landed.at[i + 1]))
        halves[i].start()
    sums[...] = jnp.zeros_like(sums)
    whole_rows.wait()
    for lat in range(lats):
        if lat in (0, split):
            halves[lat // split].wait()
        contrib = [
            jnp.dot(
                rows[lat, :, b * width : (b + 1) * width],
                weights[lat, b],
                preferred_element_type=F32,
            )
            for b in range(blocks)
        ]
        for b in range(blocks):
            sums[depart[lat, b]] += contrib[b]
    above = sums.shape[0] - rim
    first[...] = sums[pl.ds(jnp.where(odd[0] == 0, above, 0), rim)].astype(BF)
    second[...] = sums[pl.ds(jnp.where(odd[0] == 0, 0, above), rim)].astype(BF)
    mid[...] = sums[rim:above].astype(BF)


def interpolate(arrival, tiles, depart, odd):
    lats, levels, lons = arrival.shape
    blocks, width = tiles.shape[1], tiles.shape[2]
    rim = lats // 2 * blocks
    segments = lats * blocks + 2 * rim
    grid_spec = pltpu.PrefetchScalarGridSpec(
        num_scalar_prefetch=2,
        grid=(1,),
        in_specs=[ANY, ANY],
        out_specs=[VMEM, VMEM, VMEM],
        scratch_shapes=[
            pltpu.VMEM(arrival.shape, BF),
            pltpu.VMEM(tiles.shape, BF),
            pltpu.VMEM((segments, levels, width), F32),
            pltpu.SemaphoreType.DMA((3,)),
        ],
    )
    return pl.pallas_call(
        functools.partial(interpolate_kernel, rim),
        grid_spec=grid_spec,
        out_shape=[
            jax.ShapeDtypeStruct((rim, levels, width), BF),
            jax.ShapeDtypeStruct((rim, levels, width), BF),
            jax.ShapeDtypeStruct((segments - 2 * rim, levels, width), BF),
        ],
        compiler_params=pltpu.CompilerParams(vmem_limit_bytes=A_LIMIT),
        cost_estimate=pl.CostEstimate(
            flops=2 * lats * levels * lons * width,
            bytes_accessed=2 * (arrival.size + tiles.size),
            transcendentals=0,
        ),
        name="interpolate",
    )(odd, depart, arrival, tiles)


def table_kernel(lons, waves, table):
    blocks = lons // LANES
    rows = waves.shape[1]
    wave = waves[0].astype(F32)
    lane = lax.broadcasted_iota(jnp.int32, (rows, LANES), 1).astype(F32)
    product = lane * wave

    def turn(steps, period):
        left = steps - period * jnp.floor((steps + 0.5) * (1.0 / period))
        angle = left * (2.0 * math.pi / period)
        return jnp.cos(angle), jnp.sin(angle)

    fine_cos, fine_sin = turn(product, float(lons))
    coarse_cos, coarse_sin = turn(product, float(blocks))
    factor = math.sqrt(2.0 / lons)
    coarse_cos = coarse_cos * factor
    coarse_sin = coarse_sin * factor
    for b in range(blocks):
        cos_b, sin_b = coarse_cos[:, b : b + 1], coarse_sin[:, b : b + 1]
        at = slice(b * LANES, (b + 1) * LANES)
        table[0, 0, :, at] = (cos_b * fine_cos - sin_b * fine_sin).astype(BF)
        table[0, 1, :, at] = (sin_b * fine_cos + cos_b * fine_sin).astype(BF)


def wave_table(waves, lons):
    halves, count, _ = waves.shape
    rows = count
    return pl.pallas_call(
        functools.partial(table_kernel, lons),
        grid=(halves, count // rows),
        in_specs=[pl.BlockSpec((1, rows, 1), lambda h, i: (h, i, 0))],
        out_specs=pl.BlockSpec((1, 2, rows, lons), lambda h, i: (h, 0, i, 0)),
        out_shape=jax.ShapeDtypeStruct((halves, 2, count, lons), BF),
        compiler_params=pltpu.CompilerParams(vmem_limit_bytes=20 * MIB),
        cost_estimate=pl.CostEstimate(
            flops=40 * halves * count * lons, bytes_accessed=4 * halves * count * lons, transcendentals=0
        ),
        name="table",
    )(waves)


def fourier_kernel(odd, held, first, second, table, sent, grid, sums):
    levels, width = held.shape[1], held.shape[2]
    rim = first.shape[0]
    bands, lats, half, _ = sent.shape
    blocks = 2 * rim // lats
    per_row = LANES // levels
    parts = table.shape[0]
    groups = pl.cdiv(lats, per_row)

    for lat in range(groups * per_row):
        group, place = lat // per_row, lat % per_row
        for b in range(blocks):
            seg = lat * blocks + b
            if lat >= lats:
                row = jnp.zeros((levels, width), BF)
            else:
                at = seg % rim
                add = jnp.where((odd[0] == 1) == (seg < rim), first[at], second[at])
                row = (held[seg].astype(F32) + add.astype(F32)).astype(BF)
            for k in range(parts):
                start = group * LANES + (place + k) % per_row * levels
                grid[k, start : start + levels, b * width : (b + 1) * width] = row

    for k in range(parts):
        sums[k] = lax.dot_general(
            table[k], grid[k], (((1,), (1,)), ((), ())), preferred_element_type=F32
        )
    index = lax.broadcasted_iota(jnp.int32, (half, LANES), 1)
    lane = index // levels
    part = lane // 2 * 2 + index % 2
    level = index % (2 * levels) // 2
    for d in range(bands):
        for group in range(groups):
            pieces = [
                sums[k, d * half : (d + 1) * half, group * LANES : (group + 1) * LANES]
                for k in range(parts)
            ]
            for place in range(min(per_row, lats - group * per_row)):
                row = pieces[(0 - place) % per_row]
                for p in range(1, per_row):
                    row = jnp.where(lane == p, pieces[(p - place) % per_row], row)
                source = (part + place) % per_row * levels + level
                row = jnp.take_along_axis(row, source, axis=1, mode="promise_in_bounds")
                sent[d, group * per_row + place] = row.astype(BF)


def fourier(odd, held, first, second, table, bands):
    levels, width = held.shape[1], held.shape[2]
    halves, _, count, lons = table.shape
    lats = 2 * first.shape[0] * width // lons
    half = count // bands
    parts = 2 * halves
    groups = pl.cdiv(lats * levels, LANES)
    return pl.pallas_call(
        fourier_kernel,
        in_specs=[pl.BlockSpec(memory_space=pltpu.SMEM)] + [VMEM] * 4,
        out_specs=VMEM,
        out_shape=jax.ShapeDtypeStruct((bands, lats, half, LANES), BF),
        scratch_shapes=[
            pltpu.VMEM((parts, groups * LANES, lons), BF),
            pltpu.VMEM((parts, count, groups * LANES), F32),
        ],
        compiler_params=pltpu.CompilerParams(vmem_limit_bytes=14 * MIB),
        cost_estimate=pl.CostEstimate(
            flops=4 * halves * count * lons * lats * levels,
            bytes_accessed=4 * halves * count * lons,
            transcendentals=0,
        ),
        name="fourier",
    )(odd, held, first, second, table.reshape(parts, count, lons))


def turn_kernel(data, legendre, turned, table, wide, landed):
    lats, half, _ = data.shape
    copy = pltpu.make_async_copy(legendre, table, landed)
    copy.start()
    wide[...] = data[...].astype(F32).reshape(wide.shape)
    for r in range(half):
        turned[r] = wide[pl.ds(r, lats, stride=half), :].T.astype(BF)
    copy.wait()


def turn(data, legendre):
    lats, half, lanes = data.shape
    return pl.pallas_call(
        turn_kernel,
        in_specs=[VMEM, ANY],
        out_specs=[VMEM, VMEM],
        out_shape=[
            jax.ShapeDtypeStruct((half, lanes, lats), BF),
            jax.ShapeDtypeStruct(legendre.shape, BF),
        ],
        scratch_shapes=[pltpu.VMEM((lats * half, lanes), F32), pltpu.SemaphoreType.DMA],
        compiler_params=pltpu.CompilerParams(vmem_limit_bytes=T_LIMIT),
        cost_estimate=pl.CostEstimate(
            flops=0, bytes_accessed=4 * data.size + 2 * legendre.size, transcendentals=0
        ),
        name="turn",
    )(data, legendre)


def legendre_kernel(chunk, waves, lev, own, data, legendre, out, wide, staged, left):
    lats, half, lanes = data.shape
    levels = lanes // 4
    side = lanes // 2
    degrees = legendre.shape[2]
    wide[...] = data[...].astype(F32).reshape(wide.shape)
    column = lax.broadcasted_iota(jnp.int32, (lanes, degrees), 1) + lev[0] * degrees
    places = [lev[0] * levels, (1 - lev[0]) * levels]
    leaving = []
    for c in range(2):
        count = (half + 1 - c) // 2
        first = c * (half - count)

        @pl.loop(0, count // chunk)
        def _(step):
            for i in range(chunk):
                r = first + step * chunk + i
                turned = wide[pl.ds(r, lats, stride=half), :].T.astype(BF)
                for slot in range(2):
                    at = slice(slot * side, (slot + 1) * side)
                    sums = jnp.dot(
                        jnp.concatenate([own[r, at], turned[at]], axis=0),
                        legendre[2 * r + slot],
                        preferred_element_type=F32,
                    )
                    sums = jnp.where(column >= waves[2 * r + slot], sums, 0.0).astype(BF)
                    sums = sums.reshape(2, levels, 2, degrees)
                    for core in range(2):
                        staged[r, slot, pl.ds(places[core], levels)] = sums[core]

        some = slice(first, first + count)
        leaving.append(pltpu.make_async_copy(staged.at[some], out.at[some], left.at[c]))
        leaving[c].start()
    for copy in leaving:
        copy.wait()


def legendre_sums(own, other, legendre, waves, lev):
    slots, lats, degrees = legendre.shape
    half, lanes = slots // 2, other.shape[2]
    levels = lanes // 4
    chunk = 4 if half % 8 == 0 else 1
    grid_spec = pltpu.PrefetchScalarGridSpec(
        num_scalar_prefetch=2,
        grid=(1,),
        in_specs=[VMEM, VMEM, VMEM],
        out_specs=ANY,
        scratch_shapes=[
            pltpu.VMEM((lats * half, lanes), F32),
            pltpu.VMEM((half, 2, 2 * levels, 2, degrees), BF),
            pltpu.SemaphoreType.DMA((2,)),
        ],
    )
    return pl.pallas_call(
        functools.partial(legendre_kernel, chunk),
        grid_spec=grid_spec,
        out_shape=jax.ShapeDtypeStruct((half, 2, 2 * levels, 2, degrees), BF),
        compiler_params=pltpu.CompilerParams(vmem_limit_bytes=18 * MIB),
        cost_estimate=pl.CostEstimate(
            flops=2 * slots * lats * lanes * degrees,
            bytes_accessed=2 * slots * lanes * degrees,
            transcendentals=0,
        ),
        name="legendre_sums",
    )(waves, lev, own, other, legendre)


def local(arrival_adjoint, interp_tiles, departure_block, slot_wavenumber, legendre):
    lons = arrival_adjoint.shape[2]
    slots = legendre.shape[0]
    bands = lax.axis_size("band")
    lev = lax.axis_index("lev")
    odd = (lax.axis_index("band") % 2).reshape(1)
    first, second, held = interpolate(arrival_adjoint, interp_tiles, departure_block, odd)
    second = exchanged(second, [(i, i + 1) for i in range(1, bands - 1, 2)])
    first = exchanged(first, [(i, i + 1) for i in range(0, bands - 1, 2)])
    table = wave_table(slot_wavenumber.reshape(-1, 2).T[:, :, None], lons)
    sent = fourier(odd, held, first, second, table, bands)
    own = lax.all_to_all(sent, "band", split_axis=0, concat_axis=0)
    own = own.reshape(-1, *own.shape[2:])
    other = lax.ppermute(own, "lev", [(0, 1), (1, 0)])
    waves = lax.dynamic_slice_in_dim(slot_wavenumber, lax.axis_index("band") * slots, slots)
    own, legendre = turn(own, legendre)
    done = legendre_sums(own, other, legendre, waves, lev.reshape(1))
    return done.reshape(slots, done.shape[2], 2, done.shape[4])


def solution(mesh):
    placed = (
        P("band", "lev", None),
        P("band", None, None, None),
        P("band", None),
        P(),
        P("band", None, "lev"),
    )
    return jax.shard_map(
        local, mesh=mesh, in_specs=placed, out_specs=P("band", None, None, "lev"), check_vma=False
    )
```

```python
import functools
import math

import jax
import jax.numpy as jnp
from jax import lax
from jax.experimental import pallas as pl
from jax.experimental.pallas import tpu as pltpu
from jax.sharding import PartitionSpec as P

BF = jnp.bfloat16
F32 = jnp.float32
LANES = 128
MIB = 2**20
A_LIMIT = 56 * MIB
T_LIMIT = 44 * MIB
VMEM = pl.BlockSpec(memory_space=pltpu.VMEM)
ANY = pl.BlockSpec(memory_space=pl.ANY)


def exchanged(block, pairs):
    return lax.ppermute(block, "band", pairs + [(j, i) for i, j in pairs])


def interpolate_kernel(
    rim, depart, arrival, tiles, first, second, mid, rows, weights, sums, targets, landed
):
    lats, blocks, width = tiles.shape[0], tiles.shape[1], tiles.shape[2]
    cuts = [lats * i // 3 for i in range(4)]
    arriving = [
        pltpu.make_async_copy(depart, targets, landed.at[0]),
        pltpu.make_async_copy(arrival, rows, landed.at[1]),
    ]
    for i in range(3):
        some = slice(cuts[i], cuts[i + 1])
        arriving.append(
            pltpu.make_async_copy(tiles.at[some], weights.at[some], landed.at[i + 2])
        )
    for copy in arriving:
        copy.start()
    sums[...] = jnp.zeros_like(sums)
    arriving[0].wait()
    arriving[1].wait()
    for i in range(3):
        arriving[i + 2].wait()
        for lat in range(cuts[i], cuts[i + 1]):
            contrib = [
                jnp.dot(
                    rows[lat, :, b * width : (b + 1) * width],
                    weights[lat, b],
                    preferred_element_type=F32,
                )
                for b in range(blocks)
            ]
            for b in range(blocks):
                sums[targets[lat, b]] += contrib[b]
    above = sums.shape[0] - rim
    odd = lax.axis_index("band") % 2
    first[...] = sums[pl.ds(jnp.where(odd == 0, above, 0), rim)].astype(BF)
    second[...] = sums[pl.ds(jnp.where(odd == 0, 0, above), rim)].astype(BF)
    mid[...] = sums[rim:above].astype(BF)


def interpolate(arrival, tiles, depart):
    lats, levels, lons = arrival.shape
    blocks, width = tiles.shape[1], tiles.shape[2]
    rim = lats // 2 * blocks
    segments = lats * blocks + 2 * rim
    return pl.pallas_call(
        functools.partial(interpolate_kernel, rim),
        in_specs=[ANY, ANY, ANY],
        out_specs=[VMEM, VMEM, VMEM],
        out_shape=[
            jax.ShapeDtypeStruct((rim, levels, width), BF),
            jax.ShapeDtypeStruct((rim, levels, width), BF),
            jax.ShapeDtypeStruct((segments - 2 * rim, levels, width), BF),
        ],
        scratch_shapes=[
            pltpu.VMEM(arrival.shape, BF),
            pltpu.VMEM(tiles.shape, BF),
            pltpu.VMEM((segments, levels, width), F32),
            pltpu.SMEM(depart.shape, jnp.int32),
            pltpu.SemaphoreType.DMA((5,)),
        ],
        compiler_params=pltpu.CompilerParams(vmem_limit_bytes=A_LIMIT),
        cost_estimate=pl.CostEstimate(
            flops=2 * lats * levels * lons * width,
            bytes_accessed=2 * (arrival.size + tiles.size),
            transcendentals=0,
        ),
        name="interpolate",
    )(depart, arrival, tiles)


def table_kernel(lons, waves, table):
    blocks = lons // LANES
    rows = waves.shape[1]
    wave = waves[0].astype(F32)
    lane = lax.broadcasted_iota(jnp.int32, (rows, LANES), 1).astype(F32)
    product = lane * wave

    def turn(steps, period):
        left = steps - period * jnp.floor((steps + 0.5) * (1.0 / period))
        angle = left * (2.0 * math.pi / period)
        return jnp.cos(angle), jnp.sin(angle)

    fine_cos, fine_sin = turn(product, float(lons))
    coarse_cos, coarse_sin = turn(product, float(blocks))
    factor = math.sqrt(2.0 / lons)
    coarse_cos = coarse_cos * factor
    coarse_sin = coarse_sin * factor
    for b in range(blocks):
        cos_b, sin_b = coarse_cos[:, b : b + 1], coarse_sin[:, b : b + 1]
        at = slice(b * LANES, (b + 1) * LANES)
        table[0, 0, :, at] = (cos_b * fine_cos - sin_b * fine_sin).astype(BF)
        table[0, 1, :, at] = (sin_b * fine_cos + cos_b * fine_sin).astype(BF)


def wave_table(waves, lons):
    halves, count, _ = waves.shape
    rows = count
    return pl.pallas_call(
        functools.partial(table_kernel, lons),
        grid=(halves, count // rows),
        in_specs=[pl.BlockSpec((1, rows, 1), lambda h, i: (h, i, 0))],
        out_specs=pl.BlockSpec((1, 2, rows, lons), lambda h, i: (h, 0, i, 0)),
        out_shape=jax.ShapeDtypeStruct((halves, 2, count, lons), BF),
        compiler_params=pltpu.CompilerParams(vmem_limit_bytes=20 * MIB),
        cost_estimate=pl.CostEstimate(
            flops=40 * halves * count * lons, bytes_accessed=4 * halves * count * lons, transcendentals=0
        ),
        name="table",
    )(waves)


def fourier_kernel(held, first, second, table, sent, grid, sums):
    levels, width = held.shape[1], held.shape[2]
    rim = first.shape[0]
    bands, lats, half, _ = sent.shape
    odd = lax.axis_index("band") % 2
    blocks = 2 * rim // lats
    per_row = LANES // levels
    parts = table.shape[0]
    groups = pl.cdiv(lats, per_row)

    for lat in range(groups * per_row):
        group, place = lat // per_row, lat % per_row
        for b in range(blocks):
            seg = lat * blocks + b
            if lat >= lats:
                row = jnp.zeros((levels, width), BF)
            else:
                at = seg % rim
                add = jnp.where((odd == 1) == (seg < rim), first[at], second[at])
                row = (held[seg].astype(F32) + add.astype(F32)).astype(BF)
            for k in range(parts):
                start = group * LANES + (place + k) % per_row * levels
                grid[k, start : start + levels, b * width : (b + 1) * width] = row

    for k in range(parts):
        sums[k] = lax.dot_general(
            table[k], grid[k], (((1,), (1,)), ((), ())), preferred_element_type=F32
        )
    index = lax.broadcasted_iota(jnp.int32, (half, LANES), 1)
    lane = index // levels
    part = lane // 2 * 2 + index % 2
    level = index % (2 * levels) // 2
    for d in range(bands):
        for group in range(groups):
            pieces = [
                sums[k, d * half : (d + 1) * half, group * LANES : (group + 1) * LANES]
                for k in range(parts)
            ]
            for place in range(min(per_row, lats - group * per_row)):
                row = pieces[(0 - place) % per_row]
                for p in range(1, per_row):
                    row = jnp.where(lane == p, pieces[(p - place) % per_row], row)
                source = (part + place) % per_row * levels + level
                row = jnp.take_along_axis(row, source, axis=1, mode="promise_in_bounds")
                sent[d, group * per_row + place] = row.astype(BF)


def fourier(held, first, second, table, bands):
    levels, width = held.shape[1], held.shape[2]
    halves, _, count, lons = table.shape
    lats = 2 * first.shape[0] * width // lons
    half = count // bands
    parts = 2 * halves
    groups = pl.cdiv(lats * levels, LANES)
    return pl.pallas_call(
        fourier_kernel,
        in_specs=[VMEM] * 4,
        out_specs=VMEM,
        out_shape=jax.ShapeDtypeStruct((bands, lats, half, LANES), BF),
        scratch_shapes=[
            pltpu.VMEM((parts, groups * LANES, lons), BF),
            pltpu.VMEM((parts, count, groups * LANES), F32),
        ],
        compiler_params=pltpu.CompilerParams(vmem_limit_bytes=14 * MIB),
        cost_estimate=pl.CostEstimate(
            flops=4 * halves * count * lons * lats * levels,
            bytes_accessed=4 * halves * count * lons,
            transcendentals=0,
        ),
        name="fourier",
    )(held, first, second, table.reshape(parts, count, lons))


def turn_kernel(data, legendre, turned, table, wide, landed):
    lats, half, _ = data.shape
    copy = pltpu.make_async_copy(legendre, table, landed)
    copy.start()
    wide[...] = data[...].astype(F32).reshape(wide.shape)
    for r in range(half):
        turned[r] = wide[pl.ds(r, lats, stride=half), :].T.astype(BF)
    copy.wait()


def turn(data, legendre):
    lats, half, lanes = data.shape
    return pl.pallas_call(
        turn_kernel,
        in_specs=[VMEM, ANY],
        out_specs=[VMEM, VMEM],
        out_shape=[
            jax.ShapeDtypeStruct((half, lanes, lats), BF),
            jax.ShapeDtypeStruct(legendre.shape, BF),
        ],
        scratch_shapes=[pltpu.VMEM((lats * half, lanes), F32), pltpu.SemaphoreType.DMA],
        compiler_params=pltpu.CompilerParams(vmem_limit_bytes=T_LIMIT),
        cost_estimate=pl.CostEstimate(
            flops=0, bytes_accessed=4 * data.size + 2 * legendre.size, transcendentals=0
        ),
        name="turn",
    )(data, legendre)


def legendre_kernel(waves, own, data, legendre, out, wide, staged, wave, landed, left):
    lats, half, lanes = data.shape
    levels = lanes // 4
    side = lanes // 2
    degrees = legendre.shape[2]
    arriving = pltpu.make_async_copy(waves, wave, landed)
    arriving.start()
    wide[...] = data[...].astype(F32).reshape(wide.shape)
    lev = lax.axis_index("lev")
    owned = lax.axis_index("band") * 2 * half
    column = lax.broadcasted_iota(jnp.int32, (lanes, degrees), 1) + lev * degrees
    places = [lev * levels, (1 - lev) * levels]
    arriving.wait()
    leaving = []
    count = half // left.shape[0]
    for c in range(left.shape[0]):
        for r in range(c * count, (c + 1) * count):
            turned = wide[pl.ds(r, lats, stride=half), :].T.astype(BF)
            for slot in range(2):
                at = slice(slot * side, (slot + 1) * side)
                sums = jnp.dot(
                    jnp.concatenate([own[r, at], turned[at]], axis=0),
                    legendre[2 * r + slot],
                    preferred_element_type=F32,
                )
                keep = column >= wave[owned + 2 * r + slot]
                sums = jnp.where(keep, sums, 0.0).astype(BF).reshape(2, levels, 2, degrees)
                for core in range(2):
                    staged[r, slot, pl.ds(places[core], levels)] = sums[core]
        some = slice(c * count, (c + 1) * count)
        leaving.append(pltpu.make_async_copy(staged.at[some], out.at[some], left.at[c]))
        leaving[c].start()
    for copy in leaving:
        copy.wait()


def legendre_sums(own, other, legendre, waves):
    slots, lats, degrees = legendre.shape
    half, lanes = slots // 2, other.shape[2]
    levels = lanes // 4
    return pl.pallas_call(
        legendre_kernel,
        in_specs=[ANY, VMEM, VMEM, VMEM],
        out_specs=ANY,
        out_shape=jax.ShapeDtypeStruct((half, 2, 2 * levels, 2, degrees), BF),
        scratch_shapes=[
            pltpu.VMEM((lats * half, lanes), F32),
            pltpu.VMEM((half, 2, 2 * levels, 2, degrees), BF),
            pltpu.SMEM(waves.shape, jnp.int32),
            pltpu.SemaphoreType.DMA,
            pltpu.SemaphoreType.DMA((math.gcd(half, 6),)),
        ],
        compiler_params=pltpu.CompilerParams(vmem_limit_bytes=18 * MIB),
        cost_estimate=pl.CostEstimate(
            flops=2 * slots * lats * lanes * degrees,
            bytes_accessed=2 * slots * lanes * degrees,
            transcendentals=0,
        ),
        name="legendre_sums",
    )(waves, own, other, legendre)


def local(arrival_adjoint, interp_tiles, departure_block, slot_wavenumber, legendre):
    lons = arrival_adjoint.shape[2]
    slots = legendre.shape[0]
    bands = lax.axis_size("band")
    first, second, held = interpolate(arrival_adjoint, interp_tiles, departure_block)
    second = exchanged(second, [(i, i + 1) for i in range(1, bands - 1, 2)])
    first = exchanged(first, [(i, i + 1) for i in range(0, bands - 1, 2)])
    table = wave_table(slot_wavenumber.reshape(-1, 2).T[:, :, None], lons)
    sent = fourier(held, first, second, table, bands)
    own = lax.all_to_all(sent, "band", split_axis=0, concat_axis=0)
    own = own.reshape(-1, *own.shape[2:])
    other = lax.ppermute(own, "lev", [(0, 1), (1, 0)])
    own, legendre = turn(own, legendre)
    done = legendre_sums(own, other, legendre, slot_wavenumber)
    return done.reshape(slots, done.shape[2], 2, done.shape[4])


def solution(mesh):
    placed = (
        P("band", "lev", None),
        P("band", None, None, None),
        P("band", None),
        P(),
        P("band", None, "lev"),
    )
    return jax.shard_map(
        local, mesh=mesh, in_specs=placed, out_specs=P("band", None, None, "lev"), check_vma=False
    )
```

```python
import functools
import math

import jax
import jax.numpy as jnp
from jax import lax
from jax.experimental import pallas as pl
from jax.experimental.pallas import tpu as pltpu
from jax.sharding import PartitionSpec as P

BF = jnp.bfloat16
F32 = jnp.float32
LANES = 128
MIB = 2**20
A_LIMIT = 56 * MIB
T_LIMIT = 44 * MIB
F_LIMIT = 45 * MIB
W_LIMIT = 45 * MIB
COST = (10**7, 2 * 10**10)
VMEM = pl.BlockSpec(memory_space=pltpu.VMEM)
ANY = pl.BlockSpec(memory_space=pl.ANY)


def exchanged(block, pairs):
    return lax.ppermute(block, "band", pairs + [(j, i) for i, j in pairs])


def interpolate_kernel(
    rim, depart, arrival, tiles, first, second, mid, rows, weights, sums, targets, landed
):
    lats, blocks, width = tiles.shape[0], tiles.shape[1], tiles.shape[2]
    cuts = [lats * i // 3 for i in range(4)]
    arriving = [
        pltpu.make_async_copy(depart, targets, landed.at[0]),
        pltpu.make_async_copy(arrival, rows, landed.at[1]),
    ]
    for i in range(3):
        some = slice(cuts[i], cuts[i + 1])
        arriving.append(
            pltpu.make_async_copy(tiles.at[some], weights.at[some], landed.at[i + 2])
        )
    for copy in arriving:
        copy.start()
    sums[...] = jnp.zeros_like(sums)
    arriving[0].wait()
    arriving[1].wait()
    for i in range(3):
        arriving[i + 2].wait()
        for lat in range(cuts[i], cuts[i + 1]):
            contrib = [
                jnp.dot(
                    rows[lat, :, b * width : (b + 1) * width],
                    weights[lat, b],
                    preferred_element_type=F32,
                )
                for b in range(blocks)
            ]
            for b in range(blocks):
                sums[targets[lat, b]] += contrib[b]
    above = sums.shape[0] - rim
    odd = lax.axis_index("band") % 2
    first[...] = sums[pl.ds(jnp.where(odd == 0, 0, above), rim)].astype(BF)
    second[...] = sums[pl.ds(jnp.where(odd == 0, above, 0), rim)].astype(BF)
    mid[...] = sums[rim:above].astype(BF)


def interpolate(arrival, tiles, depart):
    lats, levels, lons = arrival.shape
    blocks, width = tiles.shape[1], tiles.shape[2]
    rim = lats // 2 * blocks
    segments = lats * blocks + 2 * rim
    return pl.pallas_call(
        functools.partial(interpolate_kernel, rim),
        in_specs=[ANY, ANY, ANY],
        out_specs=[VMEM, VMEM, VMEM],
        out_shape=[
            jax.ShapeDtypeStruct((rim, levels, width), BF),
            jax.ShapeDtypeStruct((rim, levels, width), BF),
            jax.ShapeDtypeStruct((segments - 2 * rim, levels, width), BF),
        ],
        scratch_shapes=[
            pltpu.VMEM(arrival.shape, BF),
            pltpu.VMEM(tiles.shape, BF),
            pltpu.VMEM((segments, levels, width), F32),
            pltpu.SMEM(depart.shape, jnp.int32),
            pltpu.SemaphoreType.DMA((5,)),
        ],
        compiler_params=pltpu.CompilerParams(vmem_limit_bytes=A_LIMIT),
        cost_estimate=pl.CostEstimate(
            flops=2 * lats * levels * lons * width,
            bytes_accessed=2 * (arrival.size + tiles.size),
            transcendentals=0,
        ),
        name="interpolate",
    )(depart, arrival, tiles)


def table_kernel(lons, waves, away, table, copied, near, columns, left):
    fetching = pltpu.make_async_copy(away, near, left.at[2])
    fetching.start()
    blocks = lons // LANES
    halves, _, rows, _ = table.shape
    lane = lax.broadcasted_iota(jnp.int32, (LANES, LANES), 1)
    on_diagonal = lane == lax.broadcasted_iota(jnp.int32, (LANES, LANES), 0)
    for i in range(waves.shape[0]):
        row = jnp.broadcast_to(waves[i : i + 1].astype(F32), (LANES, LANES))
        column = jnp.sum(jnp.where(on_diagonal, row, 0.0), axis=1, keepdims=True)
        columns[i * LANES : (i + 1) * LANES] = jnp.broadcast_to(column, (LANES, LANES))
    step = lax.broadcasted_iota(jnp.int32, (rows, LANES), 1).astype(F32)

    def turn(steps, period):
        left = steps - period * jnp.floor((steps + 0.5) * (1.0 / period))
        angle = left * (2.0 * math.pi / period)
        return jnp.cos(angle), jnp.sin(angle)

    factor = math.sqrt(2.0 / lons)
    leaving = []
    for h in range(halves):
        product = step * columns[pl.ds(h, rows, stride=halves), :]
        fine_cos, fine_sin = turn(product, float(lons))
        coarse_cos, coarse_sin = turn(product, float(blocks))
        coarse_cos = coarse_cos * factor
        coarse_sin = coarse_sin * factor
        for b in range(blocks):
            cos_b, sin_b = coarse_cos[:, b : b + 1], coarse_sin[:, b : b + 1]
            at = slice(b * LANES, (b + 1) * LANES)
            table[h, 0, :, at] = (cos_b * fine_cos - sin_b * fine_sin).astype(BF)
            table[h, 1, :, at] = (sin_b * fine_cos + cos_b * fine_sin).astype(BF)
        leaving.append(pltpu.make_async_copy(table.at[h], copied.at[h], left.at[h]))
        leaving[h].start()
    fetching.wait()
    for copy in leaving:
        copy.wait()


def wave_table(waves, lons, held):
    count = waves.shape[0] // 2
    shape = jax.ShapeDtypeStruct((2, 2, count, lons), BF)
    return pl.pallas_call(
        functools.partial(table_kernel, lons),
        in_specs=[VMEM, ANY],
        out_specs=[VMEM, ANY, VMEM],
        out_shape=[shape, shape, jax.ShapeDtypeStruct(held.shape, held.dtype)],
        scratch_shapes=[pltpu.VMEM((2 * count, LANES), F32), pltpu.SemaphoreType.DMA((3,))],
        compiler_params=pltpu.CompilerParams(vmem_limit_bytes=W_LIMIT),
        cost_estimate=pl.CostEstimate(
            flops=80 * count * lons, bytes_accessed=16 * count * lons, transcendentals=0
        ),
        name="table",
    )(waves.reshape(-1, LANES), held)


def fourier_kernel(phase, held, rims, table, sent, grid, sums):
    rim, levels, width = rims.shape
    bands, lats, half, _ = sent.shape
    odd = lax.axis_index("band") % 2
    start = jnp.where(odd == phase, 0, rim)
    blocks = rim // lats
    per_row = LANES // levels
    parts = table.shape[0]
    groups = pl.cdiv(lats, per_row)

    for lat in range(lats):
        group, place = lat // per_row, lat % per_row
        for b in range(blocks):
            seg = lat * blocks + b
            row = (held[start + seg].astype(F32) + rims[seg].astype(F32)).astype(BF)
            for k in range(parts):
                at = group * LANES + (place + k) % per_row * levels
                grid[k, at : at + levels, b * width : (b + 1) * width] = row

    for k in range(parts):
        sums[k] = lax.dot_general(
            table[k], grid[k], (((1,), (1,)), ((), ())), preferred_element_type=F32
        )
    index = lax.broadcasted_iota(jnp.int32, (half, LANES), 1)
    lane = index // levels
    part = lane // 2 * 2 + index % 2
    level = index % (2 * levels) // 2
    for d in range(bands):
        for group in range(groups):
            pieces = [
                sums[k, d * half : (d + 1) * half, group * LANES : (group + 1) * LANES]
                for k in range(parts)
            ]
            for place in range(min(per_row, lats - group * per_row)):
                row = pieces[(0 - place) % per_row]
                for p in range(1, per_row):
                    row = jnp.where(lane == p, pieces[(p - place) % per_row], row)
                source = (part + place) % per_row * levels + level
                row = jnp.take_along_axis(row, source, axis=1, mode="promise_in_bounds")
                sent[d, group * per_row + place] = row.astype(BF)


def fourier(phase, held, rims, table, bands, flops):
    rim, levels, width = rims.shape
    halves, _, count, lons = table.shape
    lats = rim * width // lons
    half = count // bands
    parts = 2 * halves
    groups = pl.cdiv(lats * levels, LANES)
    return pl.pallas_call(
        functools.partial(fourier_kernel, phase),
        in_specs=[VMEM] * 3,
        out_specs=VMEM,
        out_shape=jax.ShapeDtypeStruct((bands, lats, half, LANES), BF),
        scratch_shapes=[
            pltpu.VMEM((parts, groups * LANES, lons), BF),
            pltpu.VMEM((parts, count, groups * LANES), F32),
        ],
        compiler_params=pltpu.CompilerParams(vmem_limit_bytes=14 * MIB),
        cost_estimate=pl.CostEstimate(flops=flops, bytes_accessed=0, transcendentals=0),
        name="fourier",
    )(held, rims, table.reshape(parts, count, lons))


def lay_out(phases, wide, bands):
    lats, half, lanes = phases[0].shape
    each = lats // bands
    for b in range(bands):
        for side in range(2):
            rows = phases[side ^ (b % 2)][b * each : (b + 1) * each].astype(F32)
            at = (2 * b + side) * each * half
            wide[at : at + each * half] = rows.reshape(each * half, lanes)


def fetch_kernel(source, target, landed):
    copy = pltpu.make_async_copy(source, target, landed)
    copy.start()
    copy.wait()


def fetched(table):
    return pl.pallas_call(
        fetch_kernel,
        in_specs=[ANY],
        out_specs=VMEM,
        out_shape=jax.ShapeDtypeStruct(table.shape, table.dtype),
        scratch_shapes=[pltpu.SemaphoreType.DMA],
        compiler_params=pltpu.CompilerParams(vmem_limit_bytes=T_LIMIT),
        cost_estimate=pl.CostEstimate(flops=0, bytes_accessed=4 * table.size, transcendentals=0),
        name="fetch",
    )(table)


def turn_kernel(bands, early, late, legendre, turned, table, wide, landed):
    half, _, lats = turned.shape
    copy = pltpu.make_async_copy(legendre.at[: table.shape[0]], table, landed)
    copy.start()
    lay_out((early, late), wide, bands)
    for r in range(half):
        turned[r] = wide[pl.ds(r, lats, stride=half), :].T.astype(BF)
    copy.wait()


def turn(early, late, legendre, bands):
    lats, half, lanes = early.shape
    lats = 2 * lats
    return pl.pallas_call(
        functools.partial(turn_kernel, bands),
        in_specs=[VMEM, VMEM, ANY],
        out_specs=[VMEM, VMEM],
        out_shape=[
            jax.ShapeDtypeStruct((half, lanes, lats), BF),
            jax.ShapeDtypeStruct((legendre.shape[0] // 2, *legendre.shape[1:]), BF),
        ],
        scratch_shapes=[pltpu.VMEM((lats * half, lanes), F32), pltpu.SemaphoreType.DMA],
        compiler_params=pltpu.CompilerParams(vmem_limit_bytes=T_LIMIT),
        cost_estimate=pl.CostEstimate(
            flops=0, bytes_accessed=8 * early.size + 2 * legendre.size, transcendentals=0
        ),
        name="turn",
    )(early, late, legendre)


def legendre_kernel(
    bands, waves, own, early, late, near, legendre, out, wide, staged, far, wave, landed, left
):
    half, lanes, lats = own.shape
    levels = lanes // 4
    side = lanes // 2
    degrees = legendre.shape[2]
    split = near.shape[0]
    rest = pltpu.make_async_copy(legendre.at[split:], far, landed.at[1])
    rest.start()
    arriving = pltpu.make_async_copy(waves, wave, landed.at[0])
    arriving.start()
    lay_out((early, late), wide, bands)
    lev = lax.axis_index("lev")
    owned = lax.axis_index("band") * 2 * half
    column = lax.broadcasted_iota(jnp.int32, (lanes, degrees), 1) + lev * degrees
    places = [lev * levels, (1 - lev) * levels]
    arriving.wait()
    leaving = []
    count = half // left.shape[0]
    for c in range(left.shape[0]):
        for r in range(c * count, (c + 1) * count):
            turned = wide[pl.ds(r, lats, stride=half), :].T.astype(BF)
            if r == split // 2:
                rest.wait()
            for slot in range(2):
                at = slice(slot * side, (slot + 1) * side)
                sums = jnp.dot(
                    jnp.concatenate([own[r, at], turned[at]], axis=0),
                    (near[2 * r + slot] if 2 * r + slot < split else far[2 * r + slot - split]),
                    preferred_element_type=F32,
                )
                keep = column >= wave[owned + 2 * r + slot]
                sums = jnp.where(keep, sums, 0.0).astype(BF).reshape(2, levels, 2, degrees)
                for core in range(2):
                    staged[r, slot, pl.ds(places[core], levels)] = sums[core]
        some = slice(c * count, (c + 1) * count)
        leaving.append(pltpu.make_async_copy(staged.at[some], out.at[some], left.at[c]))
        leaving[c].start()
    for copy in leaving:
        copy.wait()


def legendre_sums(own, early, late, near, legendre, waves, bands):
    slots, lats, degrees = legendre.shape
    half, lanes = own.shape[:2]
    levels = lanes // 4
    return pl.pallas_call(
        functools.partial(legendre_kernel, bands),
        in_specs=[ANY, VMEM, VMEM, VMEM, VMEM, ANY],
        out_specs=ANY,
        out_shape=jax.ShapeDtypeStruct((half, 2, 2 * levels, 2, degrees), BF),
        scratch_shapes=[
            pltpu.VMEM((lats * half, lanes), F32),
            pltpu.VMEM((half, 2, 2 * levels, 2, degrees), BF),
            pltpu.VMEM((slots - near.shape[0], lats, degrees), BF),
            pltpu.SMEM(waves.shape, jnp.int32),
            pltpu.SemaphoreType.DMA((2,)),
            pltpu.SemaphoreType.DMA((math.gcd(half, 6),)),
        ],
        compiler_params=pltpu.CompilerParams(vmem_limit_bytes=F_LIMIT),
        cost_estimate=pl.CostEstimate(
            flops=2 * slots * lats * lanes * degrees,
            bytes_accessed=2 * slots * lanes * degrees,
            transcendentals=0,
        ),
        name="legendre_sums",
    )(waves, own, early, late, near, legendre)


def local(arrival_adjoint, interp_tiles, departure_block, slot_wavenumber, legendre):
    lons = arrival_adjoint.shape[2]
    slots = legendre.shape[0]
    bands = lax.axis_size("band")
    first, second, held = interpolate(arrival_adjoint, interp_tiles, departure_block)
    first = exchanged(first, [(i, i + 1) for i in range(1, bands - 1, 2)])
    table, copied, held = wave_table(slot_wavenumber, lons, held)
    first, second, copied = lax.optimization_barrier((first, second, copied))
    second = exchanged(second, [(i, i + 1) for i in range(0, bands - 1, 2)])

    def owned(sent):
        own = lax.all_to_all(sent, "band", split_axis=0, concat_axis=0)
        return own.reshape(-1, *own.shape[2:])

    def other(own):
        return lax.ppermute(own, "lev", [(0, 1), (1, 0)])

    sent, copied = lax.optimization_barrier(
        (fourier(0, held, first, table, bands, COST[0]), copied)
    )
    own_early = owned(sent)
    early = other(own_early)
    second, table = lax.optimization_barrier((second, fetched(copied)))
    own_late = owned(fourier(1, held, second, table, bands, COST[1]))
    late = other(own_late)
    own, near = turn(own_early, own_late, legendre, bands)
    done = legendre_sums(own, early, late, near, legendre, slot_wavenumber, bands)
    return done.reshape(slots, done.shape[2], 2, done.shape[4])


def solution(mesh):
    placed = (
        P("band", "lev", None),
        P("band", None, None, None),
        P("band", None),
        P(),
        P("band", None, "lev"),
    )
    return jax.shard_map(
        local, mesh=mesh, in_specs=placed, out_specs=P("band", None, None, "lev"), check_vma=False
    )
```
